256 devices in a mesh: clip: 16 (over y_lo, z), chan: 16 (over x, y_hi, core).
Axes of the slice: x: 4, y: 4 (y_hi: 2, y_lo: 2; y = y_hi * 2 + y_lo), z: 8, core: 2. Of those that a mesh axis runs over, the one named last changes fastest.
Arguments:
- block_in: bfloat16 [16, 512, 4, 4, 128], P('clip', 'chan'), may hold values from -6 to 6
- conv_one: bfloat16 [512, 27, 512], P('chan'), may hold values from -0.0546875 to 0.0546875
- conv_two: bfloat16 [512, 27, 512], P('chan'), may hold values from -0.0546875 to 0.0546875
- out_cotangent: bfloat16 [16, 512, 4, 4, 128], P('clip', 'chan'), may hold values from -6 to 6
Outputs:
- block_out: float32 [16, 512, 4, 4, 128], P('clip', 'chan')
- block_in_grad: float32 [16, 512, 4, 4, 128], P('clip', 'chan')
- conv_one_grad: float32 [512, 27, 512], P('chan')
- conv_two_grad: float32 [512, 27, 512], P('chan')
The draws below stay inside these ranges and needn't reach their ends.
All inputs are finite; a program needn't handle non-finite values.
Results may differ from the reference program's by a relative error of at most 0.0046.
Values may be sent and summed in bfloat16 or wider, within the bound.
No kernel may reach another device: no remote copies, remote signals or barrier semaphores. Data moves between devices by JAX's collectives and lax.ppermute only.
A program may use at most 64 MiB of HBM per device.

```python
import jax
import jax.numpy as jnp
from jax import lax

C = 512
GROUPS = 32
KTAPS = 27
FRAMES = 4
HEIGHT = 4
WIDTH = 128
CLIPS = 16


def levels(own_key, shape, cuts, low, largest):
    def one(axis_at, shards_of):
        draws = jax.random.uniform(jax.random.fold_in(jax.random.fold_in(own_key, 6), axis_at), (shards_of,), jnp.float32, low / len(cuts), largest / len(cuts))
        return jnp.repeat(jnp.exp(draws), shape[axis_at] // shards_of).reshape((-1,) + (1,) * (len(shape) - axis_at - 1))

    loudness = one(*cuts[0])
    for cut in cuts[1:]:
        loudness = loudness * one(*cut)
    return loudness


def gaussian(key, shape, scale, limit, shards=(), kind=jnp.bfloat16):
    array = scale * jax.random.normal(key, shape, jnp.float32)
    if shards:
        array = array * levels(key, shape, shards, -0.22, 0.18)
    return jnp.clip(array, -limit, limit).astype(kind)


def setup_inputs(seed: int = 0) -> dict:
    key_list = jax.random.split(jax.random.key(seed), 5)
    return {
        "block_in": gaussian(key_list[0], (CLIPS, C, FRAMES, HEIGHT, WIDTH), 1.0, 6.0, ((0, 16), (1, 16))),
        "conv_one": gaussian(key_list[1], (C, KTAPS, C), (KTAPS * C) ** -0.5, 0.0546875, ((0, 16),)),
        "conv_two": gaussian(key_list[2], (C, KTAPS, C), (KTAPS * C) ** -0.5, 0.0546875, ((0, 16),)),
        "out_cotangent": gaussian(key_list[3], (CLIPS, C, FRAMES, HEIGHT, WIDTH), 1.0, 6.0, ((0, 16), (1, 16))),
    }


def norm_act(field):
    shape = field.shape
    size = C // GROUPS
    grouped = field.reshape(shape[0], C // size, size, -1)
    center = lax.optimization_barrier(jnp.mean(grouped, axis=(2, 3), keepdims=True))
    spread = lax.optimization_barrier(jnp.mean((grouped - center) ** 2, axis=(2, 3), keepdims=True))
    normed = (grouped - center) / jnp.sqrt(spread + 1e-06)
    return jax.nn.silu(normed).reshape(shape)

def tap_list():
    return [(t_tap, h_tap, w_tap) for t_tap in range(3) for h_tap in range(3) for w_tap in range(3)]

def forward_shift(field, t_tap, h_tap, w_tap):
    padded = jnp.pad(field, ((0, 0), (0, 0), (2, 0), (1, 1), (1, 1)))
    return padded[:, :, t_tap:t_tap + FRAMES, h_tap:h_tap + HEIGHT, w_tap:w_tap + WIDTH]

def backward_shift(field, t_tap, h_tap, w_tap):
    padded = jnp.pad(field, ((0, 0), (0, 0), (0, 2), (1, 1), (1, 1)))
    return padded[:, :, 2 - t_tap:2 - t_tap + FRAMES, 2 - h_tap:2 - h_tap + HEIGHT, 2 - w_tap:2 - w_tap + WIDTH]

def conv_forward(acts, kernel):
    total = jnp.zeros(acts.shape, jnp.float32)
    for index, (t_tap, h_tap, w_tap) in enumerate(tap_list()):
        moved = forward_shift(acts, t_tap, h_tap, w_tap).astype(jnp.float32)
        total = total + jnp.einsum('oc,bcthw->bothw', kernel[:, index, :].astype(jnp.float32), moved)
    return total

def conv_input_grad(grads, kernel):
    total = jnp.zeros(grads.shape, jnp.float32)
    grads_float = grads.astype(jnp.float32)
    for index, (t_tap, h_tap, w_tap) in enumerate(tap_list()):
        term = jnp.einsum('oc,bothw->bcthw', kernel[:, index, :].astype(jnp.float32), grads_float)
        total = total + backward_shift(term, t_tap, h_tap, w_tap)
    return total

def conv_kernel_grad(acts, grads):
    grads_float = grads.astype(jnp.float32)
    pieces = []
    for t_tap, h_tap, w_tap in tap_list():
        moved = forward_shift(acts, t_tap, h_tap, w_tap).astype(jnp.float32)
        pieces.append(jnp.einsum('bothw,bcthw->oc', grads_float, moved))
    return jnp.stack(pieces, axis=1)

def reference(block_in, conv_one, conv_two, out_cotangent):
    in_float = block_in.astype(jnp.float32)
    first_float, first_pull = jax.vjp(norm_act, in_float)
    act_one = first_float.astype(jnp.bfloat16)
    hidden = conv_forward(act_one, conv_one)
    second_float, second_pull = jax.vjp(norm_act, hidden)
    act_two = second_float.astype(jnp.bfloat16)
    block_out = in_float + conv_forward(act_two, conv_two)
    conv_two_grad = conv_kernel_grad(act_two, out_cotangent)
    act_two_grad = conv_input_grad(out_cotangent, conv_two)
    hidden_grad = second_pull(act_two_grad)[0].astype(jnp.bfloat16)
    conv_one_grad = conv_kernel_grad(act_one, hidden_grad)
    act_one_grad = conv_input_grad(hidden_grad, conv_one)
    block_in_grad = out_cotangent.astype(jnp.float32) + first_pull(act_one_grad)[0]
    return (block_out, block_in_grad, conv_one_grad, conv_two_grad)
```

```python
import jax
import jax.numpy as jnp
from jax import lax
from jax.sharding import Mesh, PartitionSpec as P

GROUP = 16
XY = ("x", "yh")
CLIP = ("yl", "z")
SWAP = [(0, 1), (1, 0)]
F32 = jnp.float32
BF16 = jnp.bfloat16
TAPS = [(i, j, k) for i in range(3) for j in range(3) for k in range(3)]


def norm_act(field):
    t, h, c, w = field.shape
    grouped = field.reshape(t, h, c // GROUP, GROUP, w)
    center = jnp.mean(grouped, axis=(0, 1, 3, 4), keepdims=True)
    spread = jnp.mean((grouped - center) ** 2, axis=(0, 1, 3, 4), keepdims=True)
    normed = (grouped - center) * lax.rsqrt(spread + 1e-06)
    return jax.nn.silu(normed).reshape(field.shape)


def forward_shift(field, i, j, k):
    t, h, c, w = field.shape
    padded = jnp.pad(field, ((2, 0), (1, 1), (0, 0), (1, 1)))
    return padded[i : i + t, j : j + h, :, k : k + w]


def backward_shift(field, i, j, k):
    t, h, c, w = field.shape
    padded = jnp.pad(field, ((0, 2), (1, 1), (0, 0), (1, 1)))
    return padded[2 - i : 2 - i + t, 2 - j : 2 - j + h, :, 2 - k : 2 - k + w]


def exchange(value, axes):
    return lax.all_to_all(value, axes, 0, 0, tiled=True)


def gather_channels(local):
    core = lax.axis_index("core")
    own = exchange(jnp.broadcast_to(local[None], (8,) + local.shape), XY)
    other = lax.ppermute(own, "core", SWAP)
    first = jnp.where(core == 0, own, other)
    second = jnp.where(core == 0, other, own)
    both = jnp.stack([first, second], axis=1)
    t, h, c, w = local.shape
    return both.transpose(2, 3, 0, 1, 4, 5).reshape(t, h, 16 * c, w)


def scatter_channels(partial):
    core = lax.axis_index("core")
    t, h, c, w = partial.shape
    blocks = partial.reshape(t, h, 8, 2, c // 16, w)
    mine = jnp.where(core == 0, blocks[:, :, :, 0], blocks[:, :, :, 1])
    theirs = jnp.where(core == 0, blocks[:, :, :, 1], blocks[:, :, :, 0])
    got = lax.ppermute(theirs.astype(BF16), "core", SWAP)
    total = (mine + got.astype(F32)).astype(BF16).transpose(2, 0, 1, 3, 4)
    return jnp.sum(exchange(total, XY).astype(F32), axis=0)


def reduce_clips(grad):
    pieces = grad.astype(BF16).reshape(27, 4, 8, 4, 128).transpose(1, 3, 0, 2, 4).reshape(16, 27, 8, 128)
    own = jnp.sum(exchange(pieces, CLIP).astype(F32), axis=0).astype(BF16)
    full = exchange(jnp.broadcast_to(own[None], (16, 27, 8, 128)), CLIP)
    full = full.reshape(4, 4, 27, 8, 128).transpose(0, 3, 2, 1, 4).reshape(32, 27, 512)
    return full.astype(F32)


def conv_gathered(acts, kernel):
    products = jnp.einsum("thcw,okc->kthow", acts, kernel, preferred_element_type=F32)
    total = None
    for index, tap in enumerate(TAPS):
        moved = forward_shift(products[index], *tap)
        total = moved if total is None else total + moved
    return total


def spread_columns(grads):
    return jnp.stack([backward_shift(grads, *tap) for tap in TAPS], axis=0)


def kernel_grad(acts, columns):
    return jnp.einsum("thcw,kthow->koc", acts, columns, preferred_element_type=F32)


def input_partial(columns, kernel):
    return jnp.einsum("kthow,okc->thcw", columns, kernel, preferred_element_type=F32)


def shards(block_in, conv_one, conv_two, out_cotangent):
    x_in = block_in[0].transpose(1, 2, 0, 3)
    cot = out_cotangent[0].transpose(1, 2, 0, 3)
    in_float = x_in.astype(F32)
    first, first_pull = jax.vjp(norm_act, in_float)
    act_one = gather_channels(first.astype(BF16))
    cot_columns = spread_columns(cot)
    act_two_grad = scatter_channels(input_partial(cot_columns, conv_two))
    hidden = conv_gathered(act_one, conv_one)
    second, second_pull = jax.vjp(norm_act, hidden)
    act_two = gather_channels(second.astype(BF16))
    hidden_grad = second_pull(act_two_grad)[0].astype(BF16)
    hidden_columns = spread_columns(hidden_grad)
    one_grad = reduce_clips(kernel_grad(act_one, hidden_columns))
    act_one_grad = scatter_channels(input_partial(hidden_columns, conv_one))
    block_out = in_float + conv_gathered(act_two, conv_two)
    two_grad = reduce_clips(kernel_grad(act_two, cot_columns))
    in_grad = cot.astype(F32) + first_pull(act_one_grad)[0]
    back = lambda v: v.transpose(2, 0, 1, 3)[None]
    return back(block_out), back(in_grad), one_grad, two_grad


def solution(mesh):
    fine = Mesh(mesh.devices.reshape(2, 8, 4, 2, 2), ("yl", "z", "x", "yh", "core"))
    clip, chan = ("yl", "z"), ("x", "yh", "core")
    field = P(clip, chan, None, None, None)
    kernel = P(chan, None, None)
    return jax.shard_map(
        shards,
        mesh=fine,
        in_specs=(field, kernel, kernel, field),
        out_specs=(field, field, kernel, kernel),
        check_vma=False,
    )
```

```python
import functools

import jax
import jax.numpy as jnp
from jax import lax
from jax.experimental import pallas as pl
from jax.experimental.pallas import tpu as pltpu
from jax.sharding import Mesh, PartitionSpec as P

XY = ("x", "yh")
SWAP = [(0, 1), (1, 0)]
F32 = jnp.float32
BF16 = jnp.bfloat16
TAPS = [(i, j, k) for i in range(3) for j in range(3) for k in range(3)]
COUNT = 16 * 16 * 128
FIELD = (16, 32, 128)
SMEM_SPEC = pl.BlockSpec(memory_space=pltpu.SMEM)
VMEM_SPEC = pl.BlockSpec(memory_space=pltpu.VMEM)


def call(body, name, outs, scratch, limit, flops, *args):
    return pl.pallas_call(
        body,
        out_shape=tuple(jax.ShapeDtypeStruct(*o) for o in outs),
        in_specs=[SMEM_SPEC if a.dtype == jnp.int32 else VMEM_SPEC for a in args],
        out_specs=(VMEM_SPEC,) * len(outs),
        scratch_shapes=[pltpu.VMEM(*s) for s in scratch],
        compiler_params=pltpu.CompilerParams(vmem_limit_bytes=limit << 20),
        cost_estimate=pl.CostEstimate(flops=flops, bytes_accessed=4 << 20, transcendentals=0),
        name=name,
    )(*args)


def per_group(total):
    row = lax.broadcasted_iota(jnp.int32, (32, 128), 0)
    return jnp.where(row < 16, jnp.sum(total[:16]), jnp.sum(total[16:]))


def moments(load):
    total = load(0)
    for cell in range(1, 16):
        total = total + load(cell)
    center = per_group(total) * (1.0 / COUNT)
    total = jnp.zeros((32, 128), F32)
    for cell in range(16):
        gap = load(cell) - center
        total = total + gap * gap
    return center, lax.rsqrt(per_group(total) * (1.0 / COUNT) + 1e-06)


def act_body(field_ref, out_ref):
    center, scale = moments(lambda cell: field_ref[cell].astype(F32))
    for cell in range(16):
        normed = (field_ref[cell].astype(F32) - center) * scale
        value = (normed * jax.nn.sigmoid(normed)).astype(BF16)
        for copy in range(8):
            out_ref[copy, cell] = value


def pull_body(final, *refs):
    field_ref, pieces_ref = refs[:2]
    extra_ref = refs[2] if final else None
    out_ref, normed_ref, down_ref = refs[-3:]
    center, scale = moments(lambda cell: field_ref[cell].astype(F32))
    first = jnp.zeros((32, 128), F32)
    second = jnp.zeros((32, 128), F32)
    for cell in range(16):
        normed = (field_ref[cell].astype(F32) - center) * scale
        grad = pieces_ref[0, cell].astype(F32)
        for n in range(1, 8):
            grad = grad + pieces_ref[n, cell].astype(F32)
        gate = jax.nn.sigmoid(normed)
        down = grad * (gate * (1.0 + normed * (1.0 - gate)))
        normed_ref[cell] = normed
        down_ref[cell] = down
        first = first + down
        second = second + down * normed
    first = per_group(first) * (1.0 / COUNT)
    second = per_group(second) * (1.0 / COUNT)
    for cell in range(16):
        value = scale * (down_ref[cell] - first - normed_ref[cell] * second)
        if final:
            out_ref[cell] = extra_ref[cell].astype(F32) + value
        else:
            out_ref[cell] = value.astype(BF16)


def assemble(core_ref, own_ref, other_ref, acts):
    core = core_ref[0]

    def step(n, carry):
        low = pl.multiple_of(n * 64 + core * 32, 32)
        high = pl.multiple_of(n * 64 + 32 - core * 32, 32)
        for cell in range(16):
            columns = slice(cell % 2 * 128, cell % 2 * 128 + 128)
            acts[cell // 2, pl.ds(low, 32), columns] = own_ref[n, cell]
            acts[cell // 2, pl.ds(high, 32), columns] = other_ref[n, cell]
        return carry

    lax.fori_loop(0, 8, step, 0)


def conv_body(final, *refs):
    core_ref, own_ref, other_ref, kernel_ref = refs[:4]
    acts, products = refs[-2:]
    lane = lax.broadcasted_iota(jnp.int32, (32, 128), 1)
    assemble(core_ref, own_ref, other_ref, acts)

    def step(pair, carry):
        products[pair] = jnp.dot(kernel_ref[...], acts[pair], preferred_element_type=F32)
        return carry

    lax.fori_loop(0, 8, step, 0)

    def output(cell):
        sums = []
        for k in range(3):
            total = None
            for i in range(3):
                for j in range(3):
                    t, h = cell // 4 - 2 + i, cell % 4 - 1 + j
                    if not (0 <= t < 4 and 0 <= h < 4):
                        continue
                    source, row = t * 4 + h, (9 * i + 3 * j + k) * 32
                    left = source % 2 * 128
                    term = products[source // 2, row : row + 32, left : left + 128]
                    total = term if total is None else total + term
            sums.append(total)
        behind = jnp.where(lane == 0, 0.0, pltpu.roll(sums[0], 1, 1))
        ahead = jnp.where(lane == 127, 0.0, pltpu.roll(sums[2], 127, 1))
        return behind + sums[1] + ahead

    if final:
        extra_ref, out_ref = refs[4], refs[5]
        for cell in range(16):
            out_ref[cell] = extra_ref[cell].astype(F32) + output(cell)
    else:
        hidden_ref, out_ref = refs[4], refs[5]
        for cell in range(16):
            hidden_ref[cell] = output(cell)
        act_body(hidden_ref, out_ref)


def spread(field_ref, shifted, columns):
    lane = lax.broadcasted_iota(jnp.int32, (32, 128), 1)
    for cell in range(16):
        value = field_ref[cell].astype(F32)
        ahead = jnp.where(lane == 127, 0.0, pltpu.roll(value, 127, 1))
        behind = jnp.where(lane == 0, 0.0, pltpu.roll(value, 1, 1))
        shifted[0, cell] = ahead.astype(BF16)
        shifted[1, cell] = field_ref[cell]
        shifted[2, cell] = behind.astype(BF16)
    zero = jnp.zeros((32, 128), BF16)
    for index, (i, j, k) in enumerate(TAPS):
        for cell in range(16):
            t, h = cell // 4 + 2 - i, cell % 4 + 1 - j
            inside = 0 <= t < 4 and 0 <= h < 4
            value = shifted[k, t * 4 + h] if inside else zero
            left = cell % 2 * 128
            columns[cell // 2, index * 32 : index * 32 + 32, left : left + 128] = value


def partial_body(core_ref, field_ref, kernel_ref, mine_ref, theirs_ref, shifted, columns):
    spread(field_ref, shifted, columns)
    first = core_ref[0] == 0

    def step(pair, carry):
        out = jnp.dot(kernel_ref[...], columns[pair], preferred_element_type=F32)
        for half in range(2):
            part = out[:, half * 128 : half * 128 + 128]
            for n in range(8):
                low, high = part[n * 64 : n * 64 + 32], part[n * 64 + 32 : n * 64 + 64]
                mine_ref[n, pair * 2 + half] = jnp.where(first, low, high)
                theirs_ref[n, pair * 2 + half] = jnp.where(first, high, low).astype(BF16)
        return carry

    lax.fori_loop(0, 8, step, 0)


def grad_body(place_ref, field_ref, own_ref, other_ref, mine_ref, theirs_ref, shifted, columns, acts, total):
    spread(field_ref, shifted, columns)
    assemble(place_ref, own_ref, other_ref, acts)
    first = place_ref[1] == 0

    def step(pair, carry):
        term = lax.dot_general(
            columns[pair], acts[pair], (((1,), (1,)), ((), ())), preferred_element_type=F32
        )
        total[...] += term
        return carry

    total[...] = jnp.zeros_like(total)
    lax.fori_loop(0, 8, step, 0)
    for piece in range(8):
        left = piece % 4 * 128
        for k in range(27):
            row = k * 32 + piece // 4 * 8
            low = total[row : row + 8, left : left + 128]
            high = total[row + 16 : row + 24, left : left + 128]
            mine_ref[piece, k] = jnp.where(first, low, high)
            theirs_ref[piece, k] = jnp.where(first, high, low).astype(BF16)


FLOPS = 2 * 512 * 864 * 2048
WIDE = (8, 16, 32, 128)
PIECES = (8, 27, 8, 128)
COLUMNS = [((3,) + FIELD, BF16), ((8, 864, 256), BF16)]
ACTS = ((8, 512, 256), BF16)


def exchange(value, axes):
    return lax.all_to_all(value, axes, 0, 0, tiled=True)


def gather_channels(copies):
    own = exchange(copies, XY)
    return own, lax.ppermute(own, "core", SWAP)


def input_partial(place, field, turned):
    mine, theirs = call(partial_body, "input_partial", [(WIDE, F32), (WIDE, BF16)], COLUMNS, 16, FLOPS, place, field, turned)
    got = lax.ppermute(theirs, "core", SWAP)
    return exchange((mine + got.astype(F32)).astype(BF16), XY)


def kernel_grad(place, field, own, other):
    scratch = COLUMNS + [ACTS, ((864, 512), F32)]
    return call(grad_body, "kernel_grad", [(PIECES, F32), (PIECES, BF16)], scratch, 20, FLOPS, place, field, own, other)


def reduce_clips(pieces, first):
    mine, theirs = pieces
    got = lax.ppermute(theirs, "yl", SWAP)
    pair = (mine + got.astype(F32)).astype(BF16)
    own = jnp.sum(exchange(pair, "z").astype(F32), axis=0).astype(BF16)
    full = exchange(jnp.broadcast_to(own[None], PIECES), "z")
    other = lax.ppermute(full, "yl", SWAP)
    both = jnp.stack([jnp.where(first, full, other), jnp.where(first, other, full)])
    both = both.reshape(2, 2, 4, 27, 8, 128).transpose(0, 1, 4, 3, 2, 5).reshape(32, 27, 512)
    return both.astype(F32)


def shards(block_in, conv_one, conv_two, out_cotangent):
    cells = lambda v: v[0].transpose(1, 2, 0, 3).reshape(FIELD)
    whole = lambda v: v.reshape(4, 4, 32, 128).transpose(2, 0, 1, 3)[None]
    rows = lambda w: w.transpose(1, 0, 2).reshape(864, 512)
    core, yl = lax.axis_index("core"), lax.axis_index("yl")
    place = jnp.stack([core, yl]).astype(jnp.int32)
    x_in, cot = cells(block_in), cells(out_cotangent)
    rows_one, rows_two = rows(conv_one), rows(conv_two)

    (copies,) = call(act_body, "act_one", [(WIDE, BF16)], [], 4, 1 << 20, x_in)
    own, other = gather_channels(copies)
    pieces_two = input_partial(place, cot, rows_two.T)
    conv_scratch = [ACTS, ((8, 864, 256), F32)]
    hidden, copies_two = call(
        functools.partial(conv_body, False), "conv_one", [(FIELD, F32), (WIDE, BF16)], conv_scratch, 18, FLOPS,
        place, own, other, rows_one,
    )
    own_two, other_two = gather_channels(copies_two)
    (hidden_grad,) = call(
        functools.partial(pull_body, False), "pull_two", [(FIELD, BF16)], [(FIELD, F32)] * 2, 6, 1 << 20,
        hidden, pieces_two,
    )
    grad_one = kernel_grad(place, hidden_grad, own, other)
    pieces_one = input_partial(place, hidden_grad, rows_one.T)
    grad_two = kernel_grad(place, cot, own_two, other_two)
    (block_out,) = call(
        functools.partial(conv_body, True), "conv_two", [(FIELD, F32)], conv_scratch, 18, FLOPS,
        place, own_two, other_two, rows_two, x_in,
    )
    (in_grad,) = call(
        functools.partial(pull_body, True), "pull_one", [(FIELD, F32)], [(FIELD, F32)] * 2, 6, 1 << 20,
        x_in, pieces_one, cot,
    )
    first = yl == 0
    return whole(block_out), whole(in_grad), reduce_clips(grad_one, first), reduce_clips(grad_two, first)


def solution(mesh):
    fine = Mesh(mesh.devices.reshape(2, 8, 4, 2, 2), ("yl", "z", "x", "yh", "core"))
    clip, chan = ("yl", "z"), ("x", "yh", "core")
    field = P(clip, chan, None, None, None)
    kernel = P(chan, None, None)
    return jax.shard_map(
        shards,
        mesh=fine,
        in_specs=(field, kernel, kernel, field),
        out_specs=(field, field, kernel, kernel),
        check_vma=False,
    )
```

```python
import functools

import jax
import jax.numpy as jnp
from jax import lax
from jax.experimental import pallas as pl
from jax.experimental.pallas import tpu as pltpu
from jax.sharding import Mesh, PartitionSpec as P


XY = ("x", "yh")
SWAP = [(0, 1), (1, 0)]
F32 = jnp.float32
BF16 = jnp.bfloat16
TAPS = [(i, j, k) for i in range(3) for j in range(3) for k in range(3)]
COUNT = 16 * 16 * 128
FIELD = (16, 32, 128)
SMEM_SPEC = pl.BlockSpec(memory_space=pltpu.SMEM)
VMEM_SPEC = pl.BlockSpec(memory_space=pltpu.VMEM)


def call(body, outs, scratch, limit, flops, *args):
    return pl.pallas_call(
        body,
        out_shape=tuple(jax.ShapeDtypeStruct(*o) for o in outs),
        in_specs=[SMEM_SPEC if a.dtype == jnp.int32 else VMEM_SPEC for a in args],
        out_specs=(VMEM_SPEC,) * len(outs),
        scratch_shapes=[pltpu.VMEM(*s) for s in scratch],
        compiler_params=pltpu.CompilerParams(vmem_limit_bytes=limit << 20),
        cost_estimate=pl.CostEstimate(flops=flops, bytes_accessed=4 << 20, transcendentals=0),
    )(*args)


def per_group(total):
    row = lax.broadcasted_iota(jnp.int32, (32, 128), 0)
    return jnp.where(row < 16, jnp.sum(total[:16]), jnp.sum(total[16:]))


def moments(load):
    total = load(0)
    for cell in range(1, 16):
        total = total + load(cell)
    center = per_group(total) * (1.0 / COUNT)
    total = jnp.zeros((32, 128), F32)
    for cell in range(16):
        gap = load(cell) - center
        total = total + gap * gap
    return center, lax.rsqrt(per_group(total) * (1.0 / COUNT) + 1e-06)


def act_body(field_ref, out_ref):
    center, scale = moments(lambda cell: field_ref[cell].astype(F32))
    for cell in range(16):
        normed = (field_ref[cell].astype(F32) - center) * scale
        value = (normed * jax.nn.sigmoid(normed)).astype(BF16)
        for copy in range(8):
            out_ref[copy, cell] = value


def pull_body(count, final, *refs):
    field_ref, pieces = refs[0], refs[1 : 1 + count]
    extra_ref = refs[1 + count] if final else None
    out_ref, normed_ref, down_ref = refs[-3:]
    center, scale = moments(lambda cell: field_ref[cell].astype(F32))
    first = jnp.zeros((32, 128), F32)
    second = jnp.zeros((32, 128), F32)
    for cell in range(16):
        normed = (field_ref[cell].astype(F32) - center) * scale
        grad = None
        for n in range(8):
            piece = (pieces[0][n, cell] if count == 1 else pieces[n][cell]).astype(F32)
            grad = piece if grad is None else grad + piece
        gate = jax.nn.sigmoid(normed)
        down = grad * (gate * (1.0 + normed * (1.0 - gate)))
        normed_ref[cell] = normed
        down_ref[cell] = down
        first = first + down
        second = second + down * normed
    first = per_group(first) * (1.0 / COUNT)
    second = per_group(second) * (1.0 / COUNT)
    for cell in range(16):
        value = scale * (down_ref[cell] - first - normed_ref[cell] * second)
        if final:
            out_ref[cell] = extra_ref[cell].astype(F32) + value
        else:
            out_ref[cell] = value.astype(BF16)


def assemble(core_ref, own_ref, other_ref, acts):
    core = core_ref[0]

    def step(n, carry):
        low = pl.multiple_of(n * 64 + core * 32, 32)
        high = pl.multiple_of(n * 64 + 32 - core * 32, 32)
        for cell in range(16):
            columns = slice(cell % 2 * 128, cell % 2 * 128 + 128)
            acts[cell // 2, pl.ds(low, 32), columns] = own_ref[n, cell]
            acts[cell // 2, pl.ds(high, 32), columns] = other_ref[n, cell]
        return carry

    lax.fori_loop(0, 8, step, 0)


def conv_body(final, *refs):
    core_ref, own_ref, other_ref, kernel_ref = refs[:4]
    acts, products = refs[-2:]
    lane = lax.broadcasted_iota(jnp.int32, (32, 128), 1)
    assemble(core_ref, own_ref, other_ref, acts)

    def step(pair, carry):
        products[pair] = jnp.dot(kernel_ref[...], acts[pair], preferred_element_type=F32)
        return carry

    lax.fori_loop(0, 8, step, 0)

    def output(cell):
        sums = []
        for k in range(3):
            total = None
            for i in range(3):
                for j in range(3):
                    t, h = cell // 4 - 2 + i, cell % 4 - 1 + j
                    if not (0 <= t < 4 and 0 <= h < 4):
                        continue
                    source, row = t * 4 + h, (9 * i + 3 * j + k) * 32
                    left = source % 2 * 128
                    term = products[source // 2, row : row + 32, left : left + 128]
                    total = term if total is None else total + term
            sums.append(total)
        behind = jnp.where(lane == 0, 0.0, pltpu.roll(sums[0], 1, 1))
        ahead = jnp.where(lane == 127, 0.0, pltpu.roll(sums[2], 127, 1))
        return behind + sums[1] + ahead

    if final:
        extra_ref, out_ref = refs[4], refs[5]
        for cell in range(16):
            out_ref[cell] = extra_ref[cell].astype(F32) + output(cell)
    else:
        hidden_ref, out_ref = refs[4], refs[5]
        for cell in range(16):
            hidden_ref[cell] = output(cell)
        act_body(hidden_ref, out_ref)


def spread(field_ref, shifted, columns):
    lane = lax.broadcasted_iota(jnp.int32, (32, 128), 1)
    for cell in range(16):
        value = field_ref[cell].astype(F32)
        ahead = jnp.where(lane == 127, 0.0, pltpu.roll(value, 127, 1))
        behind = jnp.where(lane == 0, 0.0, pltpu.roll(value, 1, 1))
        shifted[0, cell] = ahead.astype(BF16)
        shifted[1, cell] = field_ref[cell]
        shifted[2, cell] = behind.astype(BF16)
    zero = jnp.zeros((32, 128), BF16)
    for index, (i, j, k) in enumerate(TAPS):
        for cell in range(16):
            t, h = cell // 4 + 2 - i, cell % 4 + 1 - j
            inside = 0 <= t < 4 and 0 <= h < 4
            value = shifted[k, t * 4 + h] if inside else zero
            left = cell % 2 * 128
            columns[cell // 2, index * 32 : index * 32 + 32, left : left + 128] = value


def partial_body(core_ref, field_ref, kernel_ref, mine_ref, theirs_ref, shifted, columns):
    spread(field_ref, shifted, columns)
    first = core_ref[0] == 0

    def step(pair, carry):
        out = jnp.dot(kernel_ref[...], columns[pair], preferred_element_type=F32)
        for half in range(2):
            part = out[:, half * 128 : half * 128 + 128]
            for n in range(8):
                low, high = part[n * 64 : n * 64 + 32], part[n * 64 + 32 : n * 64 + 64]
                mine_ref[n, pair * 2 + half] = jnp.where(first, low, high)
                theirs_ref[n, pair * 2 + half] = jnp.where(first, high, low).astype(BF16)
        return carry

    lax.fori_loop(0, 8, step, 0)


def grad_body(place_ref, field_ref, own_ref, other_ref, mine_ref, theirs_ref, shifted, columns, acts, total):
    spread(field_ref, shifted, columns)
    assemble(place_ref, own_ref, other_ref, acts)
    first = place_ref[1] == 0

    def step(pair, carry):
        term = lax.dot_general(
            columns[pair], acts[pair], (((1,), (1,)), ((), ())), preferred_element_type=F32
        )
        total[...] += term
        return carry

    total[...] = jnp.zeros_like(total)
    lax.fori_loop(0, 8, step, 0)
    for piece in range(8):
        left = piece % 4 * 128
        for k in range(27):
            row = k * 32 + piece // 4 * 8
            low = total[row : row + 8, left : left + 128]
            high = total[row + 16 : row + 24, left : left + 128]
            mine_ref[piece, k] = jnp.where(first, low, high)
            theirs_ref[piece, k] = jnp.where(first, high, low).astype(BF16)


def combine_body(place_ref, mine_ref, got_ref, *out_refs):
    here = place_ref[2]
    for k in range(8):
        x, y = lax.rem(here // 2 + k // 2, 4), lax.rem(here + k, 2)
        n = x * 2 + y
        for cell in range(16):
            out_refs[k][cell] = (mine_ref[n, cell] + got_ref[n, cell].astype(F32)).astype(BF16)


def total_body(pieces_ref, out_ref):
    for k in range(27):
        total = pieces_ref[0, k].astype(F32)
        for n in range(1, 8):
            total = total + pieces_ref[n, k].astype(F32)
        value = total.astype(BF16)
        for n in range(8):
            out_ref[n, k] = value


def finish_body(place_ref, full_ref, other_ref, out_ref):
    yl = place_ref[1]
    for piece in range(8):
        left = piece % 4 * 128
        low = pl.multiple_of((yl * 2 + piece // 4) * 8, 8)
        high = pl.multiple_of((2 - yl * 2 + piece // 4) * 8, 8)
        for k in range(27):
            out_ref[k, pl.ds(low, 8), left : left + 128] = full_ref[piece, k].astype(F32)
            out_ref[k, pl.ds(high, 8), left : left + 128] = other_ref[piece, k].astype(F32)


FLOPS = 2 * 512 * 864 * 2048
WIDE = (8, 16, 32, 128)
PIECES = (8, 27, 8, 128)
COLUMNS = [((3,) + FIELD, BF16), ((8, 864, 256), BF16)]
ACTS = ((8, 512, 256), BF16)


def exchange(value, axes):
    return lax.all_to_all(value, axes, 0, 0, tiled=True)


def swap(value, axis):
    return lax.ppermute(value, axis, SWAP)


def input_partial(place, field, turned):
    mine, theirs = call(partial_body, [(WIDE, F32), (WIDE, BF16)], COLUMNS, 16, FLOPS, place, field, turned)
    return mine, swap(theirs, "core")


def kernel_grad(place, field, own, other):
    scratch = COLUMNS + [ACTS, ((864, 512), F32)]
    mine, theirs = call(grad_body, [(PIECES, F32), (PIECES, BF16)], scratch, 20, FLOPS, place, field, own, other)
    got = swap(theirs, "yl")
    return (mine + got.astype(F32)).astype(BF16)


def reduce_clips(place, pair):
    (copies,) = call(total_body, [(PIECES, BF16)], [], 4, 1 << 20, exchange(pair, "z"))
    full = exchange(copies, "z")
    other = swap(full, "yl")
    (out,) = call(finish_body, [((27, 32, 512), F32)], [], 6, 1 << 20, place, full, other)
    return out.transpose(1, 0, 2)


def shards(block_in, conv_one, conv_two, out_cotangent):
    cells = lambda v: v[0].transpose(1, 2, 0, 3).reshape(FIELD)
    whole = lambda v: v.reshape(4, 4, 32, 128).transpose(2, 0, 1, 3)[None]
    rows = lambda w: w.transpose(1, 0, 2).reshape(864, 512)
    core, yl = lax.axis_index("core"), lax.axis_index("yl")
    place = jnp.stack([core, yl, lax.axis_index(XY)]).astype(jnp.int32)
    x_in, cot = cells(block_in), cells(out_cotangent)
    rows_one, rows_two = rows(conv_one), rows(conv_two)

    (copies,) = call(act_body, [(WIDE, BF16)], [], 4, 1 << 20, x_in)
    own = exchange(copies, XY)
    mine, got = input_partial(place, cot, rows_two.T)
    other = swap(own, "core")
    pair_two = (mine + got.astype(F32)).astype(BF16)
    pieces_two = exchange(pair_two, XY)
    conv_scratch = [ACTS, ((8, 864, 256), F32)]
    hidden, copies_two = call(
        functools.partial(conv_body, False), [(FIELD, F32), (WIDE, BF16)], conv_scratch, 18, FLOPS,
        place, own, other, rows_one,
    )
    own_two = exchange(copies_two, XY)
    (hidden_grad,) = call(
        functools.partial(pull_body, 1, False), [(FIELD, BF16)], [(FIELD, F32)] * 2, 6, 1 << 20,
        hidden, pieces_two,
    )
    grad_one = kernel_grad(place, hidden_grad, own, other)
    mine, got = input_partial(place, hidden_grad, rows_one.T)
    sends = call(combine_body, [(FIELD, BF16)] * 8, [], 10, 1 << 20, place, mine, got)
    pieces_one = [sends[0]]
    for k in range(1, 8):
        perm = [(n, (n // 2 + k // 2) % 4 * 2 + (n + k) % 2) for n in range(8)]
        pieces_one.append(lax.ppermute(sends[k], XY, perm))
    other_two = swap(own_two, "core")
    grad_two = kernel_grad(place, cot, own_two, other_two)
    out_one = reduce_clips(place, grad_one)
    out_two = reduce_clips(place, grad_two)
    (block_out,) = call(
        functools.partial(conv_body, True), [(FIELD, F32)], conv_scratch, 18, FLOPS,
        place, own_two, other_two, rows_two, x_in,
    )
    (in_grad,) = call(
        functools.partial(pull_body, 8, True), [(FIELD, F32)], [(FIELD, F32)] * 2, 6, 1 << 20,
        x_in, *pieces_one, cot,
    )
    return whole(block_out), whole(in_grad), out_one, out_two


def solution(mesh):
    fine = Mesh(mesh.devices.reshape(2, 8, 4, 2, 2), ("yl", "z", "x", "yh", "core"))
    clip, chan = ("yl", "z"), ("x", "yh", "core")
    field = P(clip, chan, None, None, None)
    kernel = P(chan, None, None)
    return jax.shard_map(
        shards,
        mesh=fine,
        in_specs=(field, kernel, kernel, field),
        out_specs=(field, field, kernel, kernel),
        check_vma=False,
    )
```

```python
import functools

import jax
import jax.numpy as jnp
from jax import lax
from jax.experimental import pallas as pl
from jax.experimental.pallas import tpu as pltpu
from jax.sharding import Mesh, PartitionSpec as P


XY = ("x", "yh")
SWAP = [(0, 1), (1, 0)]
F32 = jnp.float32
BF16 = jnp.bfloat16
TAPS = [(i, j, k) for i in range(3) for j in range(3) for k in range(3)]
COUNT = 16 * 16 * 128
FIELD = (16, 32, 128)
SMEM_SPEC = pl.BlockSpec(memory_space=pltpu.SMEM)
VMEM_SPEC = pl.BlockSpec(memory_space=pltpu.VMEM)


def call(body, outs, scratch, limit, flops, *args):
    return pl.pallas_call(
        body,
        out_shape=tuple(jax.ShapeDtypeStruct(*o) for o in outs),
        in_specs=[SMEM_SPEC if a.dtype == jnp.int32 else VMEM_SPEC for a in args],
        out_specs=(VMEM_SPEC,) * len(outs),
        scratch_shapes=[pltpu.VMEM(*s) for s in scratch],
        compiler_params=pltpu.CompilerParams(vmem_limit_bytes=limit << 20),
        cost_estimate=pl.CostEstimate(flops=flops, bytes_accessed=4 << 20, transcendentals=0),
    )(*args)


def per_group(total):
    row = lax.broadcasted_iota(jnp.int32, (32, 128), 0)
    return jnp.where(row < 16, jnp.sum(total[:16]), jnp.sum(total[16:]))


def moments(load):
    total = load(0)
    for cell in range(1, 16):
        total = total + load(cell)
    center = per_group(total) * (1.0 / COUNT)
    total = jnp.zeros((32, 128), F32)
    for cell in range(16):
        gap = load(cell) - center
        total = total + gap * gap
    return center, lax.rsqrt(per_group(total) * (1.0 / COUNT) + 1e-06)


def act_body(field_ref, out_ref):
    center, scale = moments(lambda cell: field_ref[cell].astype(F32))
    for cell in range(16):
        normed = (field_ref[cell].astype(F32) - center) * scale
        value = (normed * jax.nn.sigmoid(normed)).astype(BF16)
        for copy in range(8):
            out_ref[copy, cell] = value


def pull_body(final, *refs):
    field_ref, pieces = refs[0], refs[1:9]
    extra_ref = refs[9] if final else None
    out_ref, normed_ref, down_ref = refs[-3:]
    center, scale = moments(lambda cell: field_ref[cell].astype(F32))
    first = jnp.zeros((32, 128), F32)
    second = jnp.zeros((32, 128), F32)
    for cell in range(16):
        normed = (field_ref[cell].astype(F32) - center) * scale
        grad = None
        for n in range(8):
            piece = pieces[n][cell].astype(F32)
            grad = piece if grad is None else grad + piece
        gate = jax.nn.sigmoid(normed)
        down = grad * (gate * (1.0 + normed * (1.0 - gate)))
        normed_ref[cell] = normed
        down_ref[cell] = down
        first = first + down
        second = second + down * normed
    first = per_group(first) * (1.0 / COUNT)
    second = per_group(second) * (1.0 / COUNT)
    for cell in range(16):
        value = scale * (down_ref[cell] - first - normed_ref[cell] * second)
        if final:
            out_ref[cell] = extra_ref[cell].astype(F32) + value
        else:
            out_ref[cell] = value.astype(BF16)


def assemble(core_ref, own_ref, other_ref, acts):
    core = core_ref[0]

    def step(n, carry):
        low = pl.multiple_of(n * 64 + core * 32, 32)
        high = pl.multiple_of(n * 64 + 32 - core * 32, 32)
        for cell in range(16):
            columns = slice(cell % 2 * 128, cell % 2 * 128 + 128)
            acts[cell // 2, pl.ds(low, 32), columns] = own_ref[n, cell]
            acts[cell // 2, pl.ds(high, 32), columns] = other_ref[n, cell]
        return carry

    lax.fori_loop(0, 8, step, 0)


def conv_body(final, *refs):
    core_ref, own_ref, other_ref, kernel_ref = refs[:4]
    acts, products = refs[-2:]
    lane = lax.broadcasted_iota(jnp.int32, (32, 128), 1)
    assemble(core_ref, own_ref, other_ref, acts)

    def step(pair, carry):
        products[pair] = jnp.dot(kernel_ref[...], acts[pair], preferred_element_type=F32)
        return carry

    lax.fori_loop(0, 8, step, 0)

    def output(cell):
        sums = []
        for k in range(3):
            total = None
            for i in range(3):
                for j in range(3):
                    t, h = cell // 4 - 2 + i, cell % 4 - 1 + j
                    if not (0 <= t < 4 and 0 <= h < 4):
                        continue
                    source, row = t * 4 + h, (9 * i + 3 * j + k) * 32
                    left = source % 2 * 128
                    term = products[source // 2, row : row + 32, left : left + 128]
                    total = term if total is None else total + term
            sums.append(total)
        behind = jnp.where(lane == 0, 0.0, pltpu.roll(sums[0], 1, 1))
        ahead = jnp.where(lane == 127, 0.0, pltpu.roll(sums[2], 127, 1))
        return behind + sums[1] + ahead

    if final:
        extra_ref, out_ref = refs[4], refs[5]
        for cell in range(16):
            out_ref[cell] = extra_ref[cell].astype(F32) + output(cell)
    else:
        hidden_ref, out_ref = refs[4], refs[5]
        for cell in range(16):
            hidden_ref[cell] = output(cell)
        act_body(hidden_ref, out_ref)


def spread(field_ref, shifted, columns):
    lane = lax.broadcasted_iota(jnp.int32, (32, 128), 1)
    for cell in range(16):
        value = field_ref[cell].astype(F32)
        ahead = jnp.where(lane == 127, 0.0, pltpu.roll(value, 127, 1))
        behind = jnp.where(lane == 0, 0.0, pltpu.roll(value, 1, 1))
        shifted[0, cell] = ahead.astype(BF16)
        shifted[1, cell] = field_ref[cell]
        shifted[2, cell] = behind.astype(BF16)
    zero = jnp.zeros((32, 128), BF16)
    for index, (i, j, k) in enumerate(TAPS):
        for cell in range(16):
            t, h = cell // 4 + 2 - i, cell % 4 + 1 - j
            inside = 0 <= t < 4 and 0 <= h < 4
            value = shifted[k, t * 4 + h] if inside else zero
            left = cell % 2 * 128
            columns[cell // 2, index * 32 : index * 32 + 32, left : left + 128] = value


def partial_body(place_ref, field_ref, other_ref, kernel_ref, far_ref, *refs):
    out_refs, (shifted, columns, far_columns, result) = refs[:8], refs[8:]
    spread(field_ref, shifted, columns)
    spread(other_ref, shifted, far_columns)

    def step(pair, carry):
        out = jnp.dot(kernel_ref[...], columns[pair], preferred_element_type=F32)
        out = out + jnp.dot(far_ref[...], far_columns[pair], preferred_element_type=F32)
        for half in range(2):
            for n in range(8):
                part = out[n * 32 : n * 32 + 32, half * 128 : half * 128 + 128]
                result[n, pair * 2 + half] = part.astype(BF16)
        return carry

    lax.fori_loop(0, 8, step, 0)
    here = place_ref[2]
    for k in range(8):
        n = lax.rem(here // 2 + k // 2, 4) * 2 + lax.rem(here + k, 2)
        out_refs[k][...] = result[n]


def grad_body(place_ref, field_ref, own_ref, other_ref, mine_ref, theirs_ref, shifted, columns, acts, total):
    spread(field_ref, shifted, columns)
    assemble(place_ref, own_ref, other_ref, acts)
    first = place_ref[1] == 0

    def step(pair, carry):
        term = lax.dot_general(
            columns[pair], acts[pair], (((1,), (1,)), ((), ())), preferred_element_type=F32
        )
        total[...] += term
        return carry

    total[...] = jnp.zeros_like(total)
    lax.fori_loop(0, 8, step, 0)
    for piece in range(8):
        left = piece % 4 * 128
        for k in range(27):
            row = k * 32 + piece // 4 * 8
            low = total[row : row + 8, left : left + 128]
            high = total[row + 16 : row + 24, left : left + 128]
            mine_ref[piece, k] = jnp.where(first, low, high)
            theirs_ref[piece, k] = jnp.where(first, high, low).astype(BF16)


def total_body(pieces_ref, out_ref):
    for k in range(27):
        total = pieces_ref[0, k].astype(F32)
        for n in range(1, 8):
            total = total + pieces_ref[n, k].astype(F32)
        value = total.astype(BF16)
        for n in range(8):
            out_ref[n, k] = value


def finish_body(place_ref, full_ref, other_ref, out_ref):
    yl = place_ref[1]
    for piece in range(8):
        left = piece % 4 * 128
        low = pl.multiple_of((yl * 2 + piece // 4) * 8, 8)
        high = pl.multiple_of((2 - yl * 2 + piece // 4) * 8, 8)
        for k in range(27):
            out_ref[k, pl.ds(low, 8), left : left + 128] = full_ref[piece, k].astype(F32)
            out_ref[k, pl.ds(high, 8), left : left + 128] = other_ref[piece, k].astype(F32)


FLOPS = 2 * 512 * 864 * 2048
WIDE = (8, 16, 32, 128)
PIECES = (8, 27, 8, 128)
COLUMNS = [((3,) + FIELD, BF16), ((8, 864, 256), BF16)]
ACTS = ((8, 512, 256), BF16)


def exchange(value, axes):
    return lax.all_to_all(value, axes, 0, 0, tiled=True)


def swap(value, axis):
    return lax.ppermute(value, axis, SWAP)


def split_kernel(place, rows):
    blocks = rows.T.reshape(8, 2, 32, 864)
    first = place[0] == 0
    near = jnp.where(first, blocks[:, 0], blocks[:, 1]).reshape(256, 864)
    away = jnp.where(first, blocks[:, 1], blocks[:, 0]).reshape(256, 864)
    return near, swap(away, "core")


def input_partial(place, field, kernels):
    other = swap(field, "core")
    scratch = COLUMNS + [COLUMNS[1], (WIDE, BF16)]
    sends = call(partial_body, [(FIELD, BF16)] * 8, scratch, 16, FLOPS, place, field, other, *kernels)
    pieces = [sends[0]]
    for k in range(1, 8):
        perm = [(n, (n // 2 + k // 2) % 4 * 2 + (n + k) % 2) for n in range(8)]
        pieces.append(lax.ppermute(sends[k], XY, perm))
    return pieces


def kernel_grad(place, field, own, other):
    scratch = COLUMNS + [ACTS, ((864, 512), F32)]
    mine, theirs = call(grad_body, [(PIECES, F32), (PIECES, BF16)], scratch, 20, FLOPS, place, field, own, other)
    got = swap(theirs, "yl")
    return (mine + got.astype(F32)).astype(BF16)


def reduce_clips(place, pair):
    (copies,) = call(total_body, [(PIECES, BF16)], [], 4, 1 << 20, exchange(pair, "z"))
    full = exchange(copies, "z")
    other = swap(full, "yl")
    (out,) = call(finish_body, [((27, 32, 512), F32)], [], 6, 1 << 20, place, full, other)
    return out.transpose(1, 0, 2)


def shards(block_in, conv_one, conv_two, out_cotangent):
    cells = lambda v: v[0].transpose(1, 2, 0, 3).reshape(FIELD)
    whole = lambda v: v.reshape(4, 4, 32, 128).transpose(2, 0, 1, 3)[None]
    rows = lambda w: w.transpose(1, 0, 2).reshape(864, 512)
    core, yl = lax.axis_index("core"), lax.axis_index("yl")
    place = jnp.stack([core, yl, lax.axis_index(XY)]).astype(jnp.int32)
    x_in, cot = cells(block_in), cells(out_cotangent)
    rows_one, rows_two = rows(conv_one), rows(conv_two)

    (copies,) = call(act_body, [(WIDE, BF16)], [], 4, 1 << 20, x_in)
    own = exchange(copies, XY)
    split_two = split_kernel(place, rows_two)
    pieces_two = input_partial(place, cot, split_two)
    other = swap(own, "core")
    conv_scratch = [ACTS, ((8, 864, 256), F32)]
    hidden, copies_two = call(
        functools.partial(conv_body, False), [(FIELD, F32), (WIDE, BF16)], conv_scratch, 18, FLOPS,
        place, own, other, rows_one,
    )
    own_two = exchange(copies_two, XY)
    (hidden_grad,) = call(
        functools.partial(pull_body, False), [(FIELD, BF16)], [(FIELD, F32)] * 2, 6, 1 << 20,
        hidden, *pieces_two,
    )
    grad_one = kernel_grad(place, hidden_grad, own, other)
    split_one = split_kernel(place, rows_one)
    pieces_one = input_partial(place, hidden_grad, split_one)
    other_two = swap(own_two, "core")
    grad_two = kernel_grad(place, cot, own_two, other_two)
    out_one = reduce_clips(place, grad_one)
    out_two = reduce_clips(place, grad_two)
    (block_out,) = call(
        functools.partial(conv_body, True), [(FIELD, F32)], conv_scratch, 18, FLOPS,
        place, own_two, other_two, rows_two, x_in,
    )
    (in_grad,) = call(
        functools.partial(pull_body, True), [(FIELD, F32)], [(FIELD, F32)] * 2, 6, 1 << 20,
        x_in, *pieces_one, cot,
    )
    return whole(block_out), whole(in_grad), out_one, out_two


def solution(mesh):
    fine = Mesh(mesh.devices.reshape(2, 8, 4, 2, 2), ("yl", "z", "x", "yh", "core"))
    clip, chan = ("yl", "z"), ("x", "yh", "core")
    field = P(clip, chan, None, None, None)
    kernel = P(chan, None, None)
    return jax.shard_map(
        shards,
        mesh=fine,
        in_specs=(field, kernel, kernel, field),
        out_specs=(field, field, kernel, kernel),
        check_vma=False,
    )
```

```python
import functools

import jax
import jax.numpy as jnp
from jax import lax
from jax.experimental import pallas as pl
from jax.experimental.pallas import tpu as pltpu
from jax.sharding import Mesh, PartitionSpec as P


XY = ("x", "yh")
SWAP = [(0, 1), (1, 0)]
F32 = jnp.float32
BF16 = jnp.bfloat16
TAPS = [(i, j, k) for i in range(3) for j in range(3) for k in range(3)]
COUNT = 16 * 16 * 128
FIELD = (16, 32, 128)
SMEM_SPEC = pl.BlockSpec(memory_space=pltpu.SMEM)
VMEM_SPEC = pl.BlockSpec(memory_space=pltpu.VMEM)


def call(body, outs, scratch, limit, flops, *args):
    return pl.pallas_call(
        body,
        out_shape=tuple(jax.ShapeDtypeStruct(*o) for o in outs),
        in_specs=[SMEM_SPEC if a.dtype == jnp.int32 else VMEM_SPEC for a in args],
        out_specs=(VMEM_SPEC,) * len(outs),
        scratch_shapes=[pltpu.VMEM(*s) for s in scratch],
        compiler_params=pltpu.CompilerParams(vmem_limit_bytes=limit << 20),
        cost_estimate=pl.CostEstimate(flops=flops, bytes_accessed=4 << 20, transcendentals=0),
    )(*args)


def per_group(total):
    row = lax.broadcasted_iota(jnp.int32, (32, 128), 0)
    return jnp.where(row < 16, jnp.sum(total[:16]), jnp.sum(total[16:]))


def moments(load):
    total = load(0)
    for cell in range(1, 16):
        total = total + load(cell)
    center = per_group(total) * (1.0 / COUNT)
    total = jnp.zeros((32, 128), F32)
    for cell in range(16):
        gap = load(cell) - center
        total = total + gap * gap
    return center, lax.rsqrt(per_group(total) * (1.0 / COUNT) + 1e-06)


def act_body(field_ref, out_ref):
    center, scale = moments(lambda cell: field_ref[cell].astype(F32))
    for cell in range(16):
        normed = (field_ref[cell].astype(F32) - center) * scale
        value = (normed * jax.nn.sigmoid(normed)).astype(BF16)
        for copy in range(8):
            out_ref[copy, cell] = value


def pull_body(final, *refs):
    field_ref, pieces = refs[0], refs[1:9]
    extra_ref = refs[9] if final else None
    out_ref, normed_ref, down_ref = refs[-3:]
    center, scale = moments(lambda cell: field_ref[cell].astype(F32))
    first = jnp.zeros((32, 128), F32)
    second = jnp.zeros((32, 128), F32)
    for cell in range(16):
        normed = (field_ref[cell].astype(F32) - center) * scale
        grad = None
        for n in range(8):
            piece = pieces[n][cell].astype(F32)
            grad = piece if grad is None else grad + piece
        gate = jax.nn.sigmoid(normed)
        down = grad * (gate * (1.0 + normed * (1.0 - gate)))
        normed_ref[cell] = normed
        down_ref[cell] = down
        first = first + down
        second = second + down * normed
    first = per_group(first) * (1.0 / COUNT)
    second = per_group(second) * (1.0 / COUNT)
    for cell in range(16):
        value = scale * (down_ref[cell] - first - normed_ref[cell] * second)
        if final:
            out_ref[cell] = extra_ref[cell].astype(F32) + value
        else:
            out_ref[cell] = value.astype(BF16)


def assemble(core_ref, own_ref, other_ref, acts):
    core = core_ref[0]

    def step(n, carry):
        low = pl.multiple_of(n * 64 + core * 32, 32)
        high = pl.multiple_of(n * 64 + 32 - core * 32, 32)
        for cell in range(16):
            columns = slice(cell % 2 * 128, cell % 2 * 128 + 128)
            acts[cell // 2, pl.ds(low, 32), columns] = own_ref[n, cell]
            acts[cell // 2, pl.ds(high, 32), columns] = other_ref[n, cell]
        return carry

    lax.fori_loop(0, 8, step, 0)


def conv_body(final, *refs):
    core_ref, own_ref, other_ref, kernel_ref = refs[:4]
    acts, products = refs[-2:]
    lane = lax.broadcasted_iota(jnp.int32, (32, 128), 1)
    assemble(core_ref, own_ref, other_ref, acts)

    for pair in range(8):
        products[pair] = jnp.dot(kernel_ref[...], acts[pair], preferred_element_type=F32)

    def output(cell):
        sums = []
        for k in range(3):
            total = None
            for i in range(3):
                for j in range(3):
                    t, h = cell // 4 - 2 + i, cell % 4 - 1 + j
                    if not (0 <= t < 4 and 0 <= h < 4):
                        continue
                    source, row = t * 4 + h, (9 * i + 3 * j + k) * 32
                    left = source % 2 * 128
                    term = products[source // 2, row : row + 32, left : left + 128]
                    total = term if total is None else total + term
            sums.append(total)
        behind = jnp.where(lane == 0, 0.0, pltpu.roll(sums[0], 1, 1))
        ahead = jnp.where(lane == 127, 0.0, pltpu.roll(sums[2], 127, 1))
        return behind + sums[1] + ahead

    if final:
        extra_ref, out_ref = refs[4], refs[5]
        for cell in range(16):
            out_ref[cell] = extra_ref[cell].astype(F32) + output(cell)
    else:
        hidden_ref, out_ref = refs[4], refs[5]
        for cell in range(16):
            hidden_ref[cell] = output(cell)
        act_body(hidden_ref, out_ref)


def spread(field_ref, shifted, columns):
    lane = lax.broadcasted_iota(jnp.int32, (32, 128), 1)
    for cell in range(16):
        value = field_ref[cell].astype(F32)
        ahead = jnp.where(lane == 127, 0.0, pltpu.roll(value, 127, 1))
        behind = jnp.where(lane == 0, 0.0, pltpu.roll(value, 1, 1))
        shifted[0, cell] = ahead.astype(BF16)
        shifted[1, cell] = field_ref[cell]
        shifted[2, cell] = behind.astype(BF16)
    zero = jnp.zeros((32, 128), BF16)
    for index, (i, j, k) in enumerate(TAPS):
        for cell in range(16):
            t, h = cell // 4 + 2 - i, cell % 4 + 1 - j
            inside = 0 <= t < 4 and 0 <= h < 4
            value = shifted[k, t * 4 + h] if inside else zero
            left = cell % 2 * 128
            columns[cell // 2, index * 32 : index * 32 + 32, left : left + 128] = value


def partial_body(place_ref, field_ref, other_ref, kernel_ref, far_ref, *refs):
    out_refs, (shifted, columns, far_columns, result, near, far) = refs[:8], refs[8:]
    core = place_ref[0]
    for n in range(8):
        start = pl.multiple_of(n * 64 + core * 32, 32)
        near[n * 32 : n * 32 + 32] = kernel_ref[pl.ds(start, 32)]
        far[n * 32 : n * 32 + 32] = far_ref[pl.ds(start, 32)]
    spread(field_ref, shifted, columns)
    spread(other_ref, shifted, far_columns)
    for pair in range(8):
        out = jnp.dot(near[...], columns[pair], preferred_element_type=F32)
        out = out + jnp.dot(far[...], far_columns[pair], preferred_element_type=F32)
        for half in range(2):
            for n in range(8):
                part = out[n * 32 : n * 32 + 32, half * 128 : half * 128 + 128]
                result[n, pair * 2 + half] = part.astype(BF16)
    here = place_ref[2]
    for k in range(8):
        n = lax.rem(here // 2 + k // 2, 4) * 2 + lax.rem(here + k, 2)
        out_refs[k][...] = result[n]


def grad_body(place_ref, field_ref, own_ref, other_ref, mine_ref, theirs_ref, shifted, columns, acts, total):
    spread(field_ref, shifted, columns)
    assemble(place_ref, own_ref, other_ref, acts)
    first = place_ref[1] == 0
    for left in (0, 256):
        term = None
        for pair in range(8):
            more = lax.dot_general(
                columns[pair], acts[pair, left : left + 256], (((1,), (1,)), ((), ())), preferred_element_type=F32
            )
            term = more if term is None else term + more
        total[:, left : left + 256] = term
    for piece in range(8):
        left = piece % 4 * 128
        for k in range(27):
            row = k * 32 + piece // 4 * 8
            low = total[row : row + 8, left : left + 128]
            high = total[row + 16 : row + 24, left : left + 128]
            mine_ref[piece, k] = jnp.where(first, low, high)
            theirs_ref[piece, k] = jnp.where(first, high, low).astype(BF16)


def join_body(mine_ref, got_ref, out_ref):
    for n in range(8):
        for k in range(27):
            out_ref[n, k] = (mine_ref[n, k] + got_ref[n, k].astype(F32)).astype(BF16)


def add_pieces(pieces_ref, row):
    total = pieces_ref[0, row].astype(F32)
    for n in range(1, 8):
        total = total + pieces_ref[n, row].astype(F32)
    return total.astype(BF16)


def middle_body(pieces_ref, mine_ref, got_ref, out_ref):
    for k in range(27):
        value = add_pieces(pieces_ref, k)
        for n in range(8):
            out_ref[n, k] = value
            out_ref[n, 27 + k] = (mine_ref[n, k] + got_ref[n, k].astype(F32)).astype(BF16)


def last_body(both_ref, full_ref, out_ref):
    for k in range(27):
        value = add_pieces(both_ref, 27 + k)
        for n in range(8):
            full_ref[n, k] = both_ref[n, k]
            out_ref[n, k] = value


def finish_body(place_ref, full_ref, other_ref, out_ref):
    yl = place_ref[1]
    for piece in range(8):
        left = piece % 4 * 128
        low = pl.multiple_of((yl * 2 + piece // 4) * 8, 8)
        high = pl.multiple_of((2 - yl * 2 + piece // 4) * 8, 8)
        for k in range(27):
            out_ref[k, pl.ds(low, 8), left : left + 128] = full_ref[piece, k].astype(F32)
            out_ref[k, pl.ds(high, 8), left : left + 128] = other_ref[piece, k].astype(F32)


FLOPS = 2 * 512 * 864 * 2048
WIDE = (8, 16, 32, 128)
PIECES = (8, 27, 8, 128)
COLUMNS = [((3,) + FIELD, BF16), ((8, 864, 256), BF16)]
ACTS = ((8, 512, 256), BF16)


def exchange(value, axes):
    return lax.all_to_all(value, axes, 0, 0, tiled=True)


def swap(value, axis):
    return lax.ppermute(value, axis, SWAP)


def input_partial(place, field, rows):
    far = swap(rows, "core")
    other = swap(field, "core")
    scratch = COLUMNS + [COLUMNS[1], (WIDE, BF16), ((256, 864), BF16), ((256, 864), BF16)]
    sends = call(partial_body, [(FIELD, BF16)] * 8, scratch, 18, FLOPS, place, field, other, rows.T, far.T)
    pieces = [sends[0]]
    for k in range(1, 8):
        perm = [(n, (n // 2 + k // 2) % 4 * 2 + (n + k) % 2) for n in range(8)]
        pieces.append(lax.ppermute(sends[k], XY, perm))
    return pieces


def kernel_grad(place, field, own, other):
    scratch = COLUMNS + [ACTS, ((864, 512), F32)]
    mine, theirs = call(grad_body, [(PIECES, F32), (PIECES, BF16)], scratch, 20, FLOPS, place, field, own, other)
    return mine, swap(theirs, "yl")


def reduce_clips(place, grad_one, grad_two):
    (pair,) = call(join_body, [(PIECES, BF16)], [], 8, 1 << 20, *grad_one)
    pieces = exchange(pair, "z")
    double = (8, 54, 8, 128)
    (both,) = call(middle_body, [(double, BF16)], [], 8, 1 << 20, pieces, *grad_two)
    full_one, copies = call(last_body, [(PIECES, BF16)] * 2, [], 6, 1 << 20, exchange(both, "z"))
    full_two = exchange(copies, "z")
    outs = []
    for full in (full_one, full_two):
        other = swap(full, "yl")
        outs += call(finish_body, [((27, 32, 512), F32)], [], 6, 1 << 20, place, full, other)
    return [out.transpose(1, 0, 2) for out in outs]


def shards(block_in, conv_one, conv_two, out_cotangent):
    cells = lambda v: v[0].transpose(1, 2, 0, 3).reshape(FIELD)
    whole = lambda v: v.reshape(4, 4, 32, 128).transpose(2, 0, 1, 3)[None]
    rows = lambda w: w.transpose(1, 0, 2).reshape(864, 512)
    core, yl = lax.axis_index("core"), lax.axis_index("yl")
    place = jnp.stack([core, yl, lax.axis_index(XY)]).astype(jnp.int32)
    x_in, cot = cells(block_in), cells(out_cotangent)
    rows_two = rows(conv_two)
    rows_one = rows(conv_one)

    (copies,) = call(act_body, [(WIDE, BF16)], [], 4, 1 << 20, x_in)
    own = exchange(copies, XY)
    pieces_two = input_partial(place, cot, rows_two)
    other = swap(own, "core")
    conv_scratch = [ACTS, ((8, 864, 256), F32)]
    hidden, copies_two = call(
        functools.partial(conv_body, False), [(FIELD, F32), (WIDE, BF16)], conv_scratch, 18, FLOPS,
        place, own, other, rows_one,
    )
    own_two = exchange(copies_two, XY)
    (hidden_grad,) = call(
        functools.partial(pull_body, False), [(FIELD, BF16)], [(FIELD, F32)] * 2, 6, 1 << 20,
        hidden, *pieces_two,
    )
    grad_one = kernel_grad(place, hidden_grad, own, other)
    pieces_one = input_partial(place, hidden_grad, rows_one)
    other_two = swap(own_two, "core")
    grad_two = kernel_grad(place, cot, own_two, other_two)
    out_one, out_two = reduce_clips(place, grad_one, grad_two)
    (block_out,) = call(
        functools.partial(conv_body, True), [(FIELD, F32)], conv_scratch, 18, FLOPS,
        place, own_two, other_two, rows_two, x_in,
    )
    (in_grad,) = call(
        functools.partial(pull_body, True), [(FIELD, F32)], [(FIELD, F32)] * 2, 6, 1 << 20,
        x_in, *pieces_one, cot,
    )
    return whole(block_out), whole(in_grad), out_one, out_two


def solution(mesh):
    fine = Mesh(mesh.devices.reshape(2, 8, 4, 2, 2), ("yl", "z", "x", "yh", "core"))
    clip, chan = ("yl", "z"), ("x", "yh", "core")
    field = P(clip, chan, None, None, None)
    kernel = P(chan, None, None)
    return jax.shard_map(
        shards,
        mesh=fine,
        in_specs=(field, kernel, kernel, field),
        out_specs=(field, field, kernel, kernel),
        check_vma=False,
    )
```

```python
import functools

import jax
import jax.numpy as jnp
from jax import lax
from jax.experimental import pallas as pl
from jax.experimental.pallas import tpu as pltpu
from jax.sharding import Mesh, PartitionSpec as P


XY = ("x", "yh")
SWAP = [(0, 1), (1, 0)]
F32 = jnp.float32
BF16 = jnp.bfloat16
TAPS = [(i, j, k) for i in range(3) for j in range(3) for k in range(3)]
COUNT = 16 * 16 * 128
FIELD = (16, 32, 128)
ANY_SPEC = pl.BlockSpec(memory_space=pl.ANY)
VMEM_SPEC = pl.BlockSpec(memory_space=pltpu.VMEM)


def call(body, outs, scratch, limit, flops, *args, specs=None):
    return pl.pallas_call(
        body,
        out_shape=tuple(jax.ShapeDtypeStruct(*o) for o in outs),
        in_specs=[VMEM_SPEC] * len(args) if specs is None else specs,
        out_specs=(VMEM_SPEC,) * len(outs),
        scratch_shapes=[pltpu.VMEM(*s) if isinstance(s, tuple) else s for s in scratch],
        compiler_params=pltpu.CompilerParams(vmem_limit_bytes=limit << 20),
        cost_estimate=pl.CostEstimate(flops=flops, bytes_accessed=4 << 20, transcendentals=0),
    )(*args)


def per_group(total):
    row = lax.broadcasted_iota(jnp.int32, (32, 128), 0)
    return jnp.where(row < 16, jnp.sum(total[:16]), jnp.sum(total[16:]))


def moments(load):
    total = load(0)
    for cell in range(1, 16):
        total = total + load(cell)
    center = per_group(total) * (1.0 / COUNT)
    total = jnp.zeros((32, 128), F32)
    for cell in range(16):
        gap = load(cell) - center
        total = total + gap * gap
    return center, lax.rsqrt(per_group(total) * (1.0 / COUNT) + 1e-06)


def act_body(field_ref, out_ref):
    center, scale = moments(lambda cell: field_ref[cell].astype(F32))
    for cell in range(16):
        normed = (field_ref[cell].astype(F32) - center) * scale
        value = (normed * jax.nn.sigmoid(normed)).astype(BF16)
        for copy in range(8):
            out_ref[copy, cell] = value


def pull_body(final, *refs):
    field_ref, pieces = refs[0], refs[1:9]
    extra_ref = refs[9] if final else None
    out_ref, normed_ref, down_ref = refs[-3:]
    center, scale = moments(lambda cell: field_ref[cell].astype(F32))
    first = jnp.zeros((32, 128), F32)
    second = jnp.zeros((32, 128), F32)
    for cell in range(16):
        normed = (field_ref[cell].astype(F32) - center) * scale
        grad = None
        for n in range(8):
            piece = pieces[n][cell].astype(F32)
            grad = piece if grad is None else grad + piece
        gate = jax.nn.sigmoid(normed)
        down = grad * (gate * (1.0 + normed * (1.0 - gate)))
        normed_ref[cell] = normed
        down_ref[cell] = down
        first = first + down
        second = second + down * normed
    first = per_group(first) * (1.0 / COUNT)
    second = per_group(second) * (1.0 / COUNT)
    for cell in range(16):
        value = scale * (down_ref[cell] - first - normed_ref[cell] * second)
        if final:
            out_ref[cell] = extra_ref[cell].astype(F32) + value
        else:
            out_ref[cell] = value.astype(BF16)


def assemble(own_ref, other_ref, acts):
    core = lax.axis_index("core")

    def step(n, carry):
        low = pl.multiple_of(n * 64 + core * 32, 32)
        high = pl.multiple_of(n * 64 + 32 - core * 32, 32)
        for cell in range(16):
            columns = slice(cell % 2 * 128, cell % 2 * 128 + 128)
            acts[cell // 2, pl.ds(low, 32), columns] = own_ref[n, cell]
            acts[cell // 2, pl.ds(high, 32), columns] = other_ref[n, cell]
        return carry

    lax.fori_loop(0, 8, step, 0)


def conv_body(final, *refs):
    own_ref, other_ref, rows_ref = refs[:3]
    acts, products, kernel_ref, arrived = refs[-4:]
    fetch = pltpu.make_async_copy(rows_ref, kernel_ref, arrived)
    fetch.start()
    lane = lax.broadcasted_iota(jnp.int32, (32, 128), 1)
    assemble(own_ref, other_ref, acts)
    fetch.wait()

    for pair in range(8):
        products[pair] = jnp.dot(kernel_ref[...], acts[pair], preferred_element_type=F32)

    def output(cell):
        sums = []
        for k in range(3):
            total = None
            for i in range(3):
                for j in range(3):
                    t, h = cell // 4 - 2 + i, cell % 4 - 1 + j
                    if not (0 <= t < 4 and 0 <= h < 4):
                        continue
                    source, row = t * 4 + h, (9 * i + 3 * j + k) * 32
                    left = source % 2 * 128
                    term = products[source // 2, row : row + 32, left : left + 128]
                    total = term if total is None else total + term
            sums.append(total)
        behind = jnp.where(lane == 0, 0.0, pltpu.roll(sums[0], 1, 1))
        ahead = jnp.where(lane == 127, 0.0, pltpu.roll(sums[2], 127, 1))
        return behind + sums[1] + ahead

    if final:
        extra_ref, out_ref = refs[3], refs[4]
        for cell in range(16):
            out_ref[cell] = extra_ref[cell].astype(F32) + output(cell)
    else:
        hidden_ref, out_ref = refs[3], refs[4]
        for cell in range(16):
            hidden_ref[cell] = output(cell)
        act_body(hidden_ref, out_ref)


def spread(field_ref, shifted, columns):
    lane = lax.broadcasted_iota(jnp.int32, (32, 128), 1)
    for cell in range(16):
        value = field_ref[cell].astype(F32)
        ahead = jnp.where(lane == 127, 0.0, pltpu.roll(value, 127, 1))
        behind = jnp.where(lane == 0, 0.0, pltpu.roll(value, 1, 1))
        shifted[0, cell] = ahead.astype(BF16)
        shifted[1, cell] = field_ref[cell]
        shifted[2, cell] = behind.astype(BF16)
    zero = jnp.zeros((32, 128), BF16)
    for index, (i, j, k) in enumerate(TAPS):
        for cell in range(16):
            t, h = cell // 4 + 2 - i, cell % 4 + 1 - j
            inside = 0 <= t < 4 and 0 <= h < 4
            value = shifted[k, t * 4 + h] if inside else zero
            left = cell % 2 * 128
            columns[cell // 2, index * 32 : index * 32 + 32, left : left + 128] = value


def partial_body(field_ref, other_ref, kernel_ref, far_ref, *refs):
    out_refs, (shifted, columns, far_columns, result, near, far) = refs[:8], refs[8:]
    core = lax.axis_index("core")
    for n in range(8):
        start = pl.multiple_of(n * 64 + core * 32, 32)
        near[n * 32 : n * 32 + 32] = kernel_ref[pl.ds(start, 32)]
        far[n * 32 : n * 32 + 32] = far_ref[pl.ds(start, 32)]
    spread(field_ref, shifted, columns)
    spread(other_ref, shifted, far_columns)
    for pair in range(8):
        out = jnp.dot(near[...], columns[pair], preferred_element_type=F32)
        out = out + jnp.dot(far[...], far_columns[pair], preferred_element_type=F32)
        for half in range(2):
            for n in range(8):
                part = out[n * 32 : n * 32 + 32, half * 128 : half * 128 + 128]
                result[n, pair * 2 + half] = part.astype(BF16)
    x, y = lax.axis_index("x"), lax.axis_index("yh")
    for k in range(8):
        n = lax.rem(x + k // 2, 4) * 2 + lax.rem(y + k, 2)
        out_refs[k][...] = result[n]


def grad_body(field_ref, own_ref, other_ref, mine_ref, theirs_ref, shifted, columns, acts, total):
    spread(field_ref, shifted, columns)
    assemble(own_ref, other_ref, acts)
    first = lax.axis_index("yl") == 0
    for left in (0, 256):
        term = None
        for pair in range(8):
            more = lax.dot_general(
                columns[pair], acts[pair, left : left + 256], (((1,), (1,)), ((), ())), preferred_element_type=F32
            )
            term = more if term is None else term + more
        total[:, left : left + 256] = term
    for piece in range(8):
        left = piece % 4 * 128
        for k in range(27):
            row = k * 32 + piece // 4 * 8
            low = total[row : row + 8, left : left + 128]
            high = total[row + 16 : row + 24, left : left + 128]
            mine_ref[piece, k] = jnp.where(first, low, high)
            theirs_ref[piece, k] = jnp.where(first, high, low).astype(BF16)


def join_body(mine_ref, got_ref, out_ref):
    for n in range(8):
        for k in range(27):
            out_ref[n, k] = (mine_ref[n, k] + got_ref[n, k].astype(F32)).astype(BF16)


def add_pieces(pieces_ref, row):
    total = pieces_ref[0, row].astype(F32)
    for n in range(1, 8):
        total = total + pieces_ref[n, row].astype(F32)
    return total.astype(BF16)


def middle_body(pieces_ref, mine_ref, got_ref, out_ref):
    for k in range(27):
        value = add_pieces(pieces_ref, k)
        for n in range(8):
            out_ref[n, k] = value
            out_ref[n, 27 + k] = (mine_ref[n, k] + got_ref[n, k].astype(F32)).astype(BF16)


def last_body(both_ref, full_ref, out_ref):
    for k in range(27):
        value = add_pieces(both_ref, 27 + k)
        for n in range(8):
            full_ref[n, k] = both_ref[n, k]
            out_ref[n, k] = value


def half_body(far, pieces_ref, *refs):
    out_ref, wide, sent = refs[-3:]
    yl = lax.axis_index("yl")
    half = 1 - yl if far else yl
    for piece in range(8):
        top, left = piece // 4 * 8, piece % 4 * 128
        for k in range(27):
            wide[k, top : top + 8, left : left + 128] = pieces_ref[piece, k].astype(F32)
    put = pltpu.make_async_copy(wide, out_ref.at[:, pl.ds(pl.multiple_of(half * 16, 16), 16), :], sent)
    put.start()
    put.wait()


def finish(full, other):
    out = None
    for far, pieces in enumerate((full, other)):
        kernel = pl.pallas_call(
            functools.partial(half_body, far),
            out_shape=jax.ShapeDtypeStruct((27, 32, 512), F32),
            in_specs=[VMEM_SPEC, ANY_SPEC][: 1 + far],
            out_specs=ANY_SPEC,
            scratch_shapes=[pltpu.VMEM((27, 16, 512), F32), pltpu.SemaphoreType.DMA],
            input_output_aliases={1: 0} if far else {},
            compiler_params=pltpu.CompilerParams(vmem_limit_bytes=6 << 20),
            cost_estimate=pl.CostEstimate(flops=1 << 20, bytes_accessed=2 << 20, transcendentals=0),
        )
        out = kernel(pieces, out) if far else kernel(pieces)
    return out.transpose(1, 0, 2)


FLOPS = 2 * 512 * 864 * 2048
WIDE = (8, 16, 32, 128)
PIECES = (8, 27, 8, 128)
COLUMNS = [((3,) + FIELD, BF16), ((8, 864, 256), BF16)]
ACTS = ((8, 512, 256), BF16)


def exchange(value, axes):
    return lax.all_to_all(value, axes, 0, 0, tiled=True)


def swap(value, axis):
    return lax.ppermute(value, axis, SWAP)


def input_partial(field, rows):
    far = swap(rows, "core")
    other = swap(field, "core")
    scratch = COLUMNS + [COLUMNS[1], (WIDE, BF16), ((256, 864), BF16), ((256, 864), BF16)]
    sends = call(partial_body, [(FIELD, BF16)] * 8, scratch, 18, FLOPS, field, other, rows.T, far.T)
    pieces = [sends[0]]
    for k in range(1, 8):
        perm = [(n, (n // 2 + k // 2) % 4 * 2 + (n + k) % 2) for n in range(8)]
        pieces.append(lax.ppermute(sends[k], XY, perm))
    return pieces


def kernel_grad(field, own, other):
    scratch = COLUMNS + [ACTS, ((864, 512), F32)]
    mine, theirs = call(grad_body, [(PIECES, F32), (PIECES, BF16)], scratch, 20, FLOPS, field, own, other)
    return mine, swap(theirs, "yl")


def reduce_clips(grad_one, grad_two):
    (pair,) = call(join_body, [(PIECES, BF16)], [], 8, 1 << 20, *grad_one)
    pieces = exchange(pair, "z")
    double = (8, 54, 8, 128)
    (both,) = call(middle_body, [(double, BF16)], [], 8, 1 << 20, pieces, *grad_two)
    full_one, copies = call(last_body, [(PIECES, BF16)] * 2, [], 6, 1 << 20, exchange(both, "z"))
    full_two = exchange(copies, "z")
    outs = []
    for full in (full_one, full_two):
        outs.append(finish(full, swap(full, "yl")))
    return outs


def shards(block_in, conv_one, conv_two, out_cotangent):
    cells = lambda v: v[0].transpose(1, 2, 0, 3).reshape(FIELD)
    whole = lambda v: v.reshape(4, 4, 32, 128).transpose(2, 0, 1, 3)[None]
    rows = lambda w: w.transpose(1, 0, 2).reshape(864, 512)
    x_in, cot = cells(block_in), cells(out_cotangent)
    rows_two = rows(conv_two)
    rows_one = rows(conv_one)

    (copies,) = call(act_body, [(WIDE, BF16)], [], 4, 1 << 20, x_in)
    own = exchange(copies, XY)
    pieces_two = input_partial(cot, rows_two)
    other = swap(own, "core")
    conv_scratch = [ACTS, ((8, 864, 256), F32), ((864, 512), BF16), pltpu.SemaphoreType.DMA]
    conv_specs = [VMEM_SPEC, VMEM_SPEC, ANY_SPEC, VMEM_SPEC]
    hidden, copies_two = call(
        functools.partial(conv_body, False), [(FIELD, F32), (WIDE, BF16)], conv_scratch, 18, FLOPS,
        own, other, rows_one, specs=conv_specs[:3],
    )
    own_two = exchange(copies_two, XY)
    (hidden_grad,) = call(
        functools.partial(pull_body, False), [(FIELD, BF16)], [(FIELD, F32)] * 2, 6, 1 << 20,
        hidden, *pieces_two,
    )
    grad_one = kernel_grad(hidden_grad, own, other)
    pieces_one = input_partial(hidden_grad, rows_one)
    other_two = swap(own_two, "core")
    grad_two = kernel_grad(cot, own_two, other_two)
    out_one, out_two = reduce_clips(grad_one, grad_two)
    (block_out,) = call(
        functools.partial(conv_body, True), [(FIELD, F32)], conv_scratch, 18, FLOPS,
        own_two, other_two, rows_two, x_in, specs=conv_specs,
    )
    (in_grad,) = call(
        functools.partial(pull_body, True), [(FIELD, F32)], [(FIELD, F32)] * 2, 6, 1 << 20,
        x_in, *pieces_one, cot,
    )
    return whole(block_out), whole(in_grad), out_one, out_two


def solution(mesh):
    fine = Mesh(mesh.devices.reshape(2, 8, 4, 2, 2), ("yl", "z", "x", "yh", "core"))
    clip, chan = ("yl", "z"), ("x", "yh", "core")
    field = P(clip, chan, None, None, None)
    kernel = P(chan, None, None)
    return jax.shard_map(
        shards,
        mesh=fine,
        in_specs=(field, kernel, kernel, field),
        out_specs=(field, field, kernel, kernel),
        check_vma=False,
    )
```

```python
import functools

import jax
import jax.numpy as jnp
from jax import lax
from jax.experimental import pallas as pl
from jax.experimental.pallas import tpu as pltpu
from jax.sharding import Mesh, PartitionSpec as P


XY = ("x", "yh")
SWAP = [(0, 1), (1, 0)]
RINGS = [[z * 2 for z in range(8)], [(z + 4) % 8 * 2 + 1 for z in range(8)]]
F32 = jnp.float32
BF16 = jnp.bfloat16
TAPS = [(i, j, k) for i in range(3) for j in range(3) for k in range(3)]
COUNT = 16 * 16 * 128
FIELD = (16, 32, 128)
ANY_SPEC = pl.BlockSpec(memory_space=pl.ANY)
VMEM_SPEC = pl.BlockSpec(memory_space=pltpu.VMEM)


def call(body, outs, scratch, limit, flops, *args, specs=None):
    return pl.pallas_call(
        body,
        out_shape=tuple(jax.ShapeDtypeStruct(*o) for o in outs),
        in_specs=[VMEM_SPEC] * len(args) if specs is None else specs,
        out_specs=(VMEM_SPEC,) * len(outs),
        scratch_shapes=[pltpu.VMEM(*s) if isinstance(s, tuple) else s for s in scratch],
        compiler_params=pltpu.CompilerParams(vmem_limit_bytes=limit << 20),
        cost_estimate=pl.CostEstimate(flops=flops, bytes_accessed=4 << 20, transcendentals=0),
    )(*args)


def per_group(total):
    row = lax.broadcasted_iota(jnp.int32, (32, 128), 0)
    return jnp.where(row < 16, jnp.sum(total[:16]), jnp.sum(total[16:]))


def moments(load):
    total = load(0)
    for cell in range(1, 16):
        total = total + load(cell)
    center = per_group(total) * (1.0 / COUNT)
    total = jnp.zeros((32, 128), F32)
    for cell in range(16):
        gap = load(cell) - center
        total = total + gap * gap
    return center, lax.rsqrt(per_group(total) * (1.0 / COUNT) + 1e-06)


def act_body(field_ref, out_ref):
    center, scale = moments(lambda cell: field_ref[cell].astype(F32))
    for cell in range(16):
        normed = (field_ref[cell].astype(F32) - center) * scale
        value = (normed * jax.nn.sigmoid(normed)).astype(BF16)
        for copy in range(8):
            out_ref[copy, cell] = value


def pull_body(final, *refs):
    field_ref, pieces = refs[0], refs[1:9]
    extra_ref = refs[9] if final else None
    out_ref, normed_ref, down_ref = refs[-3:]
    center, scale = moments(lambda cell: field_ref[cell].astype(F32))
    first = jnp.zeros((32, 128), F32)
    second = jnp.zeros((32, 128), F32)
    for cell in range(16):
        normed = (field_ref[cell].astype(F32) - center) * scale
        grad = None
        for n in range(8):
            piece = pieces[n][cell].astype(F32)
            grad = piece if grad is None else grad + piece
        gate = jax.nn.sigmoid(normed)
        down = grad * (gate * (1.0 + normed * (1.0 - gate)))
        normed_ref[cell] = normed
        down_ref[cell] = down
        first = first + down
        second = second + down * normed
    first = per_group(first) * (1.0 / COUNT)
    second = per_group(second) * (1.0 / COUNT)
    for cell in range(16):
        value = scale * (down_ref[cell] - first - normed_ref[cell] * second)
        if final:
            out_ref[cell] = extra_ref[cell].astype(F32) + value
        else:
            out_ref[cell] = value.astype(BF16)


def assemble(own_ref, other_ref, acts):
    core = lax.axis_index("core")

    def step(n, carry):
        low = pl.multiple_of(n * 64 + core * 32, 32)
        high = pl.multiple_of(n * 64 + 32 - core * 32, 32)
        for cell in range(16):
            columns = slice(cell % 2 * 128, cell % 2 * 128 + 128)
            acts[cell // 2, pl.ds(low, 32), columns] = own_ref[n, cell]
            acts[cell // 2, pl.ds(high, 32), columns] = other_ref[n, cell]
        return carry

    lax.fori_loop(0, 8, step, 0)


def conv_body(final, *refs):
    own_ref, other_ref, rows_ref = refs[:3]
    acts, products, kernel_ref, arrived = refs[-4:]
    fetch = pltpu.make_async_copy(rows_ref, kernel_ref, arrived)
    fetch.start()
    lane = lax.broadcasted_iota(jnp.int32, (32, 128), 1)
    assemble(own_ref, other_ref, acts)
    fetch.wait()

    for pair in range(8):
        products[pair] = jnp.dot(kernel_ref[...], acts[pair], preferred_element_type=F32)

    def output(cell):
        sums = []
        for k in range(3):
            total = None
            for i in range(3):
                for j in range(3):
                    t, h = cell // 4 - 2 + i, cell % 4 - 1 + j
                    if not (0 <= t < 4 and 0 <= h < 4):
                        continue
                    source, row = t * 4 + h, (9 * i + 3 * j + k) * 32
                    left = source % 2 * 128
                    term = products[source // 2, row : row + 32, left : left + 128]
                    total = term if total is None else total + term
            sums.append(total)
        behind = jnp.where(lane == 0, 0.0, pltpu.roll(sums[0], 1, 1))
        ahead = jnp.where(lane == 127, 0.0, pltpu.roll(sums[2], 127, 1))
        return behind + sums[1] + ahead

    if final:
        extra_ref, out_ref = refs[3], refs[4]
        for cell in range(16):
            out_ref[cell] = extra_ref[cell].astype(F32) + output(cell)
    else:
        hidden_ref, out_ref = refs[3], refs[4]
        for cell in range(16):
            hidden_ref[cell] = output(cell)
        act_body(hidden_ref, out_ref)


def spread(field_ref, shifted, columns):
    lane = lax.broadcasted_iota(jnp.int32, (32, 128), 1)
    for cell in range(16):
        value = field_ref[cell].astype(F32)
        ahead = jnp.where(lane == 127, 0.0, pltpu.roll(value, 127, 1))
        behind = jnp.where(lane == 0, 0.0, pltpu.roll(value, 1, 1))
        shifted[0, cell] = ahead.astype(BF16)
        shifted[1, cell] = field_ref[cell]
        shifted[2, cell] = behind.astype(BF16)
    zero = jnp.zeros((32, 128), BF16)
    for index, (i, j, k) in enumerate(TAPS):
        for cell in range(16):
            t, h = cell // 4 + 2 - i, cell % 4 + 1 - j
            inside = 0 <= t < 4 and 0 <= h < 4
            value = shifted[k, t * 4 + h] if inside else zero
            left = cell % 2 * 128
            columns[cell // 2, index * 32 : index * 32 + 32, left : left + 128] = value


def partial_body(field_ref, other_ref, kernel_ref, far_ref, *refs):
    out_refs, (shifted, columns, far_columns, result, near, far) = refs[:8], refs[8:]
    core = lax.axis_index("core")
    for n in range(8):
        start = pl.multiple_of(n * 64 + core * 32, 32)
        near[n * 32 : n * 32 + 32] = kernel_ref[pl.ds(start, 32)]
        far[n * 32 : n * 32 + 32] = far_ref[pl.ds(start, 32)]
    spread(field_ref, shifted, columns)
    spread(other_ref, shifted, far_columns)
    for pair in range(8):
        out = jnp.dot(near[...], columns[pair], preferred_element_type=F32)
        out = out + jnp.dot(far[...], far_columns[pair], preferred_element_type=F32)
        for half in range(2):
            for n in range(8):
                part = out[n * 32 : n * 32 + 32, half * 128 : half * 128 + 128]
                result[n, pair * 2 + half] = part.astype(BF16)
    x, y = lax.axis_index("x"), lax.axis_index("yh")
    for k in range(8):
        n = lax.rem(x + k // 2, 4) * 2 + lax.rem(y + k, 2)
        out_refs[k][...] = result[n]


def grad_body(field_ref, own_ref, other_ref, mine_ref, theirs_ref, shifted, columns, acts, total):
    spread(field_ref, shifted, columns)
    assemble(own_ref, other_ref, acts)
    first = lax.axis_index("yl") == 0
    for left in (0, 256):
        term = None
        for pair in range(8):
            more = lax.dot_general(
                columns[pair], acts[pair, left : left + 256], (((1,), (1,)), ((), ())), preferred_element_type=F32
            )
            term = more if term is None else term + more
        total[:, left : left + 256] = term
    for piece in range(8):
        left = piece % 4 * 128
        for k in range(27):
            row = k * 32 + piece // 4 * 8
            low = total[row : row + 8, left : left + 128]
            high = total[row + 16 : row + 24, left : left + 128]
            mine_ref[piece, k] = jnp.where(first, low, high)
            theirs_ref[piece, k] = jnp.where(first, high, low).astype(BF16)


def join_body(mine_ref, got_ref, out_ref):
    for n in range(8):
        for k in range(27):
            out_ref[n, k] = (mine_ref[n, k] + got_ref[n, k].astype(F32)).astype(BF16)


def add_pieces(pieces_ref, row):
    total = pieces_ref[0, row].astype(F32)
    for n in range(1, 8):
        total = total + pieces_ref[n, row].astype(F32)
    return total.astype(BF16)


def middle_body(pieces_ref, mine_ref, got_ref, out_ref):
    for k in range(27):
        value = add_pieces(pieces_ref, k)
        for n in range(8):
            out_ref[n, k] = value
            out_ref[n, 27 + k] = (mine_ref[n, k] + got_ref[n, k].astype(F32)).astype(BF16)


def last_body(both_ref, full_ref, out_ref):
    for k in range(27):
        value = add_pieces(both_ref, 27 + k)
        for n in range(8):
            full_ref[n, k] = both_ref[n, k]
            out_ref[n, k] = value


def half_body(far, pieces_ref, *refs):
    out_ref, wide, sent = refs[-3:]
    yl = lax.axis_index("yl")
    half = 1 - yl if far else yl
    for piece in range(8):
        top, left = piece // 4 * 8, piece % 4 * 128
        for k in range(27):
            wide[k, top : top + 8, left : left + 128] = pieces_ref[piece, k].astype(F32)
    put = pltpu.make_async_copy(wide, out_ref.at[:, pl.ds(pl.multiple_of(half * 16, 16), 16), :], sent)
    put.start()
    put.wait()


def finish(full, other):
    out = None
    for far, pieces in enumerate((full, other)):
        kernel = pl.pallas_call(
            functools.partial(half_body, far),
            out_shape=jax.ShapeDtypeStruct((27, 32, 512), F32),
            in_specs=[VMEM_SPEC, ANY_SPEC][: 1 + far],
            out_specs=ANY_SPEC,
            scratch_shapes=[pltpu.VMEM((27, 16, 512), F32), pltpu.SemaphoreType.DMA],
            input_output_aliases={1: 0} if far else {},
            compiler_params=pltpu.CompilerParams(vmem_limit_bytes=6 << 20),
            cost_estimate=pl.CostEstimate(flops=1 << 20, bytes_accessed=2 << 20, transcendentals=0),
        )
        out = kernel(pieces, out) if far else kernel(pieces)
    return out.transpose(1, 0, 2)


FLOPS = 2 * 512 * 864 * 2048
WIDE = (8, 16, 32, 128)
PIECES = (8, 27, 8, 128)
COLUMNS = [((3,) + FIELD, BF16), ((8, 864, 256), BF16)]
ACTS = ((8, 512, 256), BF16)


def exchange(value, axes):
    groups = RINGS if axes == "z" else None
    axes = ("z", "core") if axes == "z" else axes
    return lax.all_to_all(value, axes, 0, 0, axis_index_groups=groups, tiled=True)


def swap(value, axis):
    return lax.ppermute(value, axis, SWAP)


def input_partial(field, rows):
    far = swap(rows, "core")
    other = swap(field, "core")
    scratch = COLUMNS + [COLUMNS[1], (WIDE, BF16), ((256, 864), BF16), ((256, 864), BF16)]
    sends = call(partial_body, [(FIELD, BF16)] * 8, scratch, 18, FLOPS, field, other, rows.T, far.T)
    pieces = [sends[0]]
    for k in range(1, 8):
        perm = [(n, (n // 2 + k // 2) % 4 * 2 + (n + k) % 2) for n in range(8)]
        pieces.append(lax.ppermute(sends[k], XY, perm))
    return pieces


def kernel_grad(field, own, other):
    scratch = COLUMNS + [ACTS, ((864, 512), F32)]
    mine, theirs = call(grad_body, [(PIECES, F32), (PIECES, BF16)], scratch, 20, FLOPS, field, own, other)
    return mine, swap(theirs, "yl")


def reduce_clips(grad_one, grad_two):
    (pair,) = call(join_body, [(PIECES, BF16)], [], 8, 1 << 20, *grad_one)
    pieces = exchange(pair, "z")
    double = (8, 54, 8, 128)
    (both,) = call(middle_body, [(double, BF16)], [], 8, 1 << 20, pieces, *grad_two)
    full_one, copies = call(last_body, [(PIECES, BF16)] * 2, [], 6, 1 << 20, exchange(both, "z"))
    full_two = exchange(copies, "z")
    outs = []
    for full in (full_one, full_two):
        outs.append(finish(full, swap(full, "yl")))
    return outs


def shards(block_in, conv_one, conv_two, out_cotangent):
    cells = lambda v: v[0].transpose(1, 2, 0, 3).reshape(FIELD)
    whole = lambda v: v.reshape(4, 4, 32, 128).transpose(2, 0, 1, 3)[None]
    rows = lambda w: w.transpose(1, 0, 2).reshape(864, 512)
    x_in, cot = cells(block_in), cells(out_cotangent)
    rows_two = rows(conv_two)
    rows_one = rows(conv_one)

    (copies,) = call(act_body, [(WIDE, BF16)], [], 4, 1 << 20, x_in)
    own = exchange(copies, XY)
    pieces_two = input_partial(cot, rows_two)
    other = swap(own, "core")
    conv_scratch = [ACTS, ((8, 864, 256), F32), ((864, 512), BF16), pltpu.SemaphoreType.DMA]
    conv_specs = [VMEM_SPEC, VMEM_SPEC, ANY_SPEC, VMEM_SPEC]
    hidden, copies_two = call(
        functools.partial(conv_body, False), [(FIELD, F32), (WIDE, BF16)], conv_scratch, 18, FLOPS,
        own, other, rows_one, specs=conv_specs[:3],
    )
    own_two = exchange(copies_two, XY)
    (hidden_grad,) = call(
        functools.partial(pull_body, False), [(FIELD, BF16)], [(FIELD, F32)] * 2, 6, 1 << 20,
        hidden, *pieces_two,
    )
    grad_one = kernel_grad(hidden_grad, own, other)
    pieces_one = input_partial(hidden_grad, rows_one)
    other_two = swap(own_two, "core")
    grad_two = kernel_grad(cot, own_two, other_two)
    out_one, out_two = reduce_clips(grad_one, grad_two)
    (block_out,) = call(
        functools.partial(conv_body, True), [(FIELD, F32)], conv_scratch, 18, FLOPS,
        own_two, other_two, rows_two, x_in, specs=conv_specs,
    )
    (in_grad,) = call(
        functools.partial(pull_body, True), [(FIELD, F32)], [(FIELD, F32)] * 2, 6, 1 << 20,
        x_in, *pieces_one, cot,
    )
    return whole(block_out), whole(in_grad), out_one, out_two


def solution(mesh):
    fine = Mesh(mesh.devices.reshape(2, 8, 4, 2, 2), ("yl", "z", "x", "yh", "core"))
    clip, chan = ("yl", "z"), ("x", "yh", "core")
    field = P(clip, chan, None, None, None)
    kernel = P(chan, None, None)
    return jax.shard_map(
        shards,
        mesh=fine,
        in_specs=(field, kernel, kernel, field),
        out_specs=(field, field, kernel, kernel),
        check_vma=False,
    )
```
